32 devices in a mesh: row: 2 (over y), col: 16 (over z, x, core).
Axes of the slice: x: 2, y: 2, z: 4, core: 2. Of those that a mesh axis runs over, the one named last changes fastest.
Arguments:
- eigen_slab: float32 [2048, 16384], P('row', 'col'), may hold values from -6 to 6
- secular_poles: float32 [32768], P('col'), may hold values from 0 to 4, as said below
- coupling: float32 [32768], P('col'), may hold values from -7 to 7
- window_roots: float32 [128], replicated, may hold values from 0 to 4, as said below
- deflated: int32 [32768], P('col'), may hold values 0 or 1
- column_map: int32 [32768], P('col'), may hold values from 0 to 32767, as said below
Outputs:
- vectors: float32 [2048, 128], P(('row', 'col'))
The draws below stay inside these ranges and needn't reach their ends.
Inputs may be any that keep to these rules, and one draw needn't show every extreme that they name: `column_map`: A permutation of the 32768 columns. Grid column c holds columns c * 1024 to (c + 1) * 1024 - 1 and 16384 + c * 1024 to 16384 + (c + 1) * 1024 - 1 of the slab, and positions c * 2048 to (c + 1) * 2048 - 1. Of one grid column's positions, exactly 256 map to the columns of one grid column, 128 to each of 14 others, none to the remaining one. `secular_poles`: each pole lies between (k + 0.2) * 4 / 64 and (k + 0.8) * 4 / 64 for a whole number k. `window_roots`: each root lies within 0.15 * 4 / 64 of k * 4 / 64 for a whole number k of 1 to 63.
All inputs are finite; a program needn't handle non-finite values. No bound on the sum of `deflated` on one device may be relied on, other than what follows from the above.
Results may differ from the reference program's by a relative error of at most 0.0003.
Values sent between devices are 32-bit elements; how exact they have to be, the bound alone decides.
No kernel may reach another device: no remote copies, remote signals or barrier semaphores. Data moves between devices by JAX's collectives and lax.ppermute only.
A program may use at most 64 MiB of HBM per device.

```python
import jax
import jax.numpy as jnp
from jax import lax

COLS_DEV = 1024
WIN = 128
HALF = 16384
ORDER = 32768
POS_DEV = 2048
ROWS = 2048
SLOTS = 64
SHARE = 128
CAP = 256


def draw_secular_poles(key, part):
    slot_key, spread_key = jax.random.split(jax.random.fold_in(key, 101), 2)
    slot_ids = jax.random.randint(slot_key, (ORDER,), 0, SLOTS).astype(jnp.float32)
    offset = jax.random.uniform(spread_key, (ORDER,), jnp.float32, -1.0, 1.0)
    return (slot_ids + 0.5 + 0.3 * offset) * (4.0 / SLOTS)


def draw_window_roots(key, part):
    slot_key, spread_key = jax.random.split(jax.random.fold_in(key, 202), 2)
    slot_ids = jax.random.randint(slot_key, (WIN,), 1, SLOTS).astype(jnp.float32)
    offset = jax.random.uniform(spread_key, (WIN,), jnp.float32, -0.15, 0.15)
    return (slot_ids + offset) * (4.0 / SLOTS)


def draw_coupling(key, part):
    value_key = jax.random.fold_in(key, 303)
    position = jnp.arange(ORDER, dtype=jnp.float32) / ORDER
    values = jax.random.truncated_normal(value_key, -4.0, 4.0, (ORDER,), jnp.float32)
    growth = 1.0 + 0.75 * position
    return values * growth


def draw_column_map(key, part):
    shift_key, source_key, target_key = jax.random.split(jax.random.fold_in(key, 404), 3)
    groups = ORDER // POS_DEV
    shifts = jax.random.permutation(shift_key, groups)[:groups - 1]
    slot_range = jnp.arange(POS_DEV, dtype=jnp.int32)
    group_of = jnp.where(slot_range < CAP, 0, 1 + (slot_range - CAP) // SHARE)
    source_order = jax.vmap(lambda sub_key: jax.random.permutation(sub_key, POS_DEV))(jax.random.split(source_key, groups))
    target_order = jax.vmap(lambda sub_key: jax.random.permutation(sub_key, POS_DEV))(jax.random.split(target_key, groups))
    source_dev = jnp.arange(groups, dtype=jnp.int32)[:, None]
    target_dev = (source_dev + shifts[group_of][None, :]) % groups
    local_target = target_order[target_dev, slot_range[None, :]]
    column = jnp.where(local_target < COLS_DEV, target_dev * COLS_DEV + local_target, HALF + target_dev * COLS_DEV + local_target - COLS_DEV)
    positions = source_dev * POS_DEV + source_order
    result = jnp.zeros((ORDER,), jnp.int32).at[positions.reshape(-1)].set(column.reshape(-1).astype(jnp.int32))
    return result.astype(jnp.int32)


def touch_ends(values, stream_key, low, high):
    extent = values.shape
    index_at = [jax.random.randint(jax.random.fold_in(stream_key, axis), (), 0, extent[axis]) for axis in range(len(extent))]
    values = values.at[tuple(index_at)].set(low)
    longest = extent.index(max(extent))
    index_at[longest] = (index_at[longest] + 1) % extent[longest]
    return values.at[tuple(index_at)].set(high)


def shard_levels(own_key, extent, shards, smallest, largest):
    def one(dim, blocks):
        steps = jax.random.uniform(jax.random.fold_in(jax.random.fold_in(own_key, 6), dim), (blocks,), jnp.float32, smallest / len(shards), largest / len(shards))
        return jnp.repeat(jnp.exp(steps), extent[dim] // blocks).reshape((-1,) + (1,) * (len(extent) - dim - 1))

    loudness = one(*shards[0])
    for cut in shards[1:]:
        loudness = loudness * one(*cut)
    return loudness


def bell_draw(rng, dims, deviation, limit, shards=(), kind=jnp.bfloat16):
    values = deviation * jax.random.normal(rng, dims, jnp.float32)
    if shards:
        values = values * shard_levels(rng, dims, shards, -0.22, 0.18)
    return jnp.clip(values, -limit, limit).astype(kind)


def setup_inputs(seed: int = 0) -> dict:
    seeds = jax.random.split(jax.random.key(seed), 7)
    return {
        "eigen_slab": bell_draw(seeds[0], (ROWS, HALF), 1.0, 6.0, ((0, 2), (1, 16)), jnp.float32),
        "secular_poles": draw_secular_poles(jax.random.fold_in(seeds[6], 71), 0),
        "coupling": draw_coupling(jax.random.fold_in(seeds[6], 71), 0),
        "window_roots": draw_window_roots(jax.random.fold_in(seeds[6], 71), 0),
        "deflated": touch_ends((jax.random.randint(seeds[4], (ORDER,), 0, 4) < 1).astype(jnp.int32), jax.random.fold_in(seeds[4], 1), 0, 1),
        "column_map": draw_column_map(jax.random.fold_in(seeds[6], 71), 0),
    }


def reference(eigen_slab, secular_poles, coupling, window_roots, deflated, column_map):
    distance = secular_poles[:, None] - window_roots[None, :]
    entries = jnp.where(deflated[:, None] == 0, coupling[:, None] / distance, jnp.zeros_like(distance))
    inverse = lax.rsqrt(lax.optimization_barrier(jnp.sum(entries * entries, axis=0)))
    scaled = entries * inverse[None, :]
    placed = jnp.zeros_like(scaled).at[column_map.astype(jnp.int32)].set(scaled)
    upper_part = jnp.dot(eigen_slab[:ROWS // 2], placed[:HALF], precision=lax.Precision.HIGHEST, preferred_element_type=jnp.float32)
    lower_part = jnp.dot(eigen_slab[ROWS // 2:], placed[HALF:], precision=lax.Precision.HIGHEST, preferred_element_type=jnp.float32)
    return jnp.concatenate([upper_part, lower_part], axis=0)
```

```python
import functools

import jax
import jax.numpy as jnp
from jax import lax
from jax.experimental import pallas as pl
from jax.experimental.pallas import tpu as pltpu
from jax.sharding import PartitionSpec as P

LANES = 128
SUBLANES = 8
F32 = jnp.float32
BF16 = jnp.bfloat16
NT = (((1,), (1,)), ((), ()))


def log2(n):
    assert n > 0 and n & (n - 1) == 0
    return n.bit_length() - 1


def bit_reverse(value, bits):
    out = jnp.zeros_like(value)
    for b in range(bits):
        out = out | (((value >> b) & 1) << (bits - 1 - b))
    return out


def pieces_of(value, count):
    out = []
    for _ in range(count):
        piece = value.astype(BF16)
        out.append(piece)
        value = value - piece.astype(F32)
    return out


def place_kernel(
    half_ref, me_ref, map_ref, coupling_ref, poles_ref, deflated_ref, send_ref, keep_ref, *, groups, cols_dev
):
    chunks = map_ref.shape[0]
    rows_dev = cols_dev // LANES
    total = groups * rows_dev
    within = map_ref[...] - half_ref[0] * (groups * cols_dev)
    valid = (within >= 0) & (within < groups * cols_dev)
    target = (within >> log2(cols_dev)) & (groups - 1)
    place = bit_reverse(target ^ me_ref[0], log2(groups))
    row = place * rows_dev + ((within >> log2(LANES)) & (rows_dev - 1))
    row = jnp.where(valid, row, -1)
    lane = within & (LANES - 1)
    live = jnp.where(deflated_ref[...] == 0, coupling_ref[...], 0.0)
    pieces = [p.astype(F32) for p in pieces_of(live, 3) + pieces_of(poles_ref[...], 3)]
    row_ids = lax.broadcasted_iota(jnp.int32, (total, LANES), 0)
    lane_ids = lax.broadcasted_iota(jnp.int32, (LANES, LANES), 0)
    left = [[] for _ in pieces]
    right = []
    for c in range(chunks):
        hit = row_ids == row[c : c + 1]
        for k, piece in enumerate(pieces):
            left[k].append(jnp.where(hit, piece[c : c + 1], 0.0).astype(BF16))
        right.append(jnp.where(lane_ids == lane[c : c + 1], 1.0, 0.0).astype(BF16))
    right = jnp.concatenate(right, axis=1)
    left = jnp.concatenate([jnp.concatenate(part, axis=1) for part in left], axis=0)
    dense = lax.dot_general(left, right, NT, preferred_element_type=F32).reshape(6, total, LANES)
    z = (dense[0] + dense[1] + dense[2]).reshape(2, groups // 2, rows_dev, LANES)
    d = (dense[3] + dense[4] + dense[5]).reshape(2, groups // 2, rows_dev, LANES)
    keep_ref[:, :rows_dev, :] = z[0]
    keep_ref[:, rows_dev:, :] = d[0]
    send_ref[:, :rows_dev, :] = z[1]
    send_ref[:, rows_dev:, :] = d[1]


def prepare_kernel(slab_ref, roots_ref, coupling_ref, poles_ref, deflated_ref, hi_ref, lo_ref, roots_t_ref, squares_ref):
    slab = slab_ref[...]
    hi = slab.astype(BF16)
    hi_ref[...] = hi
    lo_ref[...] = (slab - hi.astype(F32)).astype(BF16)

    @pl.when(pl.program_id(0) == 0)
    def _():
        window = roots_ref.shape[1]
        roots_t = jnp.broadcast_to(roots_ref[...], (LANES, window)).T
        roots_t_ref[...] = roots_t
        live = jnp.where(deflated_ref[...] == 0, coupling_ref[...], 0.0)
        poles = poles_ref[...]
        total = jnp.zeros((window, LANES), F32)
        for c in range(live.shape[0]):
            entry = live[c : c + 1] / (poles[c : c + 1] - roots_t)
            total = total + entry * entry
        squares_ref[...] = jnp.broadcast_to(jnp.sum(total.T, axis=0, keepdims=True), squares_ref.shape)


def product_kernel(me_ref, zd_ref, roots_t_ref, hi_ref, lo_ref, send_ref, keep_ref, *, groups):
    rows_dev = zd_ref.shape[0] // 2
    window = roots_t_ref.shape[0]
    parts = []
    for c in range(rows_dev):
        parts.append(zd_ref[c : c + 1, :] / (zd_ref[rows_dev + c : rows_dev + c + 1, :] - roots_t_ref[...]))
    entries = jnp.concatenate(parts, axis=1)
    factor = jnp.concatenate(pieces_of(entries, 2), axis=0)
    block = hi_ref.shape[0] // groups
    for ref, lead in ((send_ref, 1), (keep_ref, 0)):
        for m in range(groups // 2):
            place = lead * (groups // 2) + m
            rel = int(format(place, f"0{log2(groups)}b")[::-1], 2)
            start = pl.multiple_of((me_ref[0] ^ rel) * block, block)
            rows = pl.ds(start, block)
            out = lax.dot_general(hi_ref[rows, :], factor, NT, preferred_element_type=F32)
            low = lax.dot_general(lo_ref[rows, :], factor, NT, preferred_element_type=F32)
            out = out + low
            ref[m * block : (m + 1) * block, :] = out[:, :window] + out[:, window:]


def exchange(value, groups, bit):
    return lax.ppermute(value, "col", [(i, i ^ bit) for i in range(groups)])


def body(eigen_slab, secular_poles, coupling, window_roots, deflated, column_map):
    groups = lax.axis_size("col")
    row_groups = lax.axis_size("row")
    rows, cols_dev = eigen_slab.shape
    window = window_roots.shape[0]
    bits = log2(groups)
    half = (lax.axis_index("row") >= row_groups // 2).astype(jnp.int32).reshape(1)
    me = lax.axis_index("col").astype(jnp.int32).reshape(1)
    tiled = lambda a: a.reshape(-1, LANES)
    rows_dev = cols_dev // LANES
    smem = pl.BlockSpec(memory_space=pltpu.SMEM)
    vmem = pl.BlockSpec(memory_space=pltpu.VMEM)

    placed = jax.ShapeDtypeStruct((groups // 2, 2 * rows_dev, LANES), F32)
    send, keep = pl.pallas_call(
        functools.partial(place_kernel, groups=groups, cols_dev=cols_dev),
        out_shape=(placed, placed),
        in_specs=[smem, smem, vmem, vmem, vmem, vmem],
        out_specs=(vmem, vmem),
        name="place",
    )(half, me, tiled(column_map), tiled(coupling), tiled(secular_poles), tiled(deflated))

    step = 128
    flat = lambda shape: pl.BlockSpec(shape, lambda i: (0, 0))
    hi, lo, roots_t, squares = pl.pallas_call(
        prepare_kernel,
        grid=(rows // step,),
        out_shape=(
            jax.ShapeDtypeStruct((rows, cols_dev), BF16),
            jax.ShapeDtypeStruct((rows, cols_dev), BF16),
            jax.ShapeDtypeStruct((window, LANES), F32),
            jax.ShapeDtypeStruct((SUBLANES, window), F32),
        ),
        in_specs=[
            pl.BlockSpec((step, cols_dev), lambda i: (i, 0)),
            flat((1, window)),
            flat(tiled(coupling).shape),
            flat(tiled(coupling).shape),
            flat(tiled(coupling).shape),
        ],
        out_specs=(
            pl.BlockSpec((step, cols_dev), lambda i: (i, 0)),
            pl.BlockSpec((step, cols_dev), lambda i: (i, 0)),
            flat((window, LANES)),
            flat((SUBLANES, window)),
        ),
        name="prepare",
    )(eigen_slab, window_roots.reshape(1, window), tiled(coupling), tiled(secular_poles), tiled(deflated))

    value = keep + exchange(send, groups, 1)
    for b in range(1, bits):
        mid = value.shape[0] // 2
        value = value[:mid] + exchange(value[mid:], groups, 1 << b)

    half_rows = jax.ShapeDtypeStruct((rows // 2, window), F32)
    send, keep = pl.pallas_call(
        functools.partial(product_kernel, groups=groups),
        out_shape=(half_rows, half_rows),
        in_specs=[smem, vmem, vmem, vmem, vmem],
        out_specs=(vmem, vmem),
        name="product",
    )(me, value.reshape(2 * rows_dev, LANES), roots_t, hi, lo)

    for b in range(bits):
        got = exchange(jnp.concatenate([send, squares]), groups, 1 << b)
        mid = send.shape[0]
        keep = keep + got[:mid]
        squares = squares + got[mid:]
        if b + 1 < bits:
            keep, send = keep[: mid // 2], keep[mid // 2 :]
    return keep * lax.rsqrt(squares[:1])


def solution(mesh):
    return jax.shard_map(
        body,
        mesh=mesh,
        in_specs=(P("row", "col"), P("col"), P("col"), P(), P("col"), P("col")),
        out_specs=P(("row", "col"), None),
        check_vma=False,
    )
```

```python
import functools

import jax
import jax.numpy as jnp
from jax import lax
from jax.experimental import pallas as pl
from jax.experimental.pallas import tpu as pltpu
from jax.sharding import PartitionSpec as P


LANES = 128
SUBLANES = 8
F32 = jnp.float32
BF16 = jnp.bfloat16
NT = (((1,), (1,)), ((), ()))
PARAMS = pltpu.CompilerParams(vmem_limit_bytes=24 * 2**20)


def log2(n):
    assert n > 0 and n & (n - 1) == 0
    return n.bit_length() - 1


def bit_reverse(value, bits):
    out = jnp.zeros_like(value)
    for b in range(bits):
        out = out | (((value >> b) & 1) << (bits - 1 - b))
    return out


def pieces_of(value, count):
    out = []
    for _ in range(count):
        piece = value.astype(BF16)
        out.append(piece)
        value = value - piece.astype(F32)
    return out


def place_kernel(
    half_ref,
    me_ref,
    map_hbm,
    coupling_hbm,
    deflated_hbm,
    poles_hbm,
    roots_hbm,
    slab_hbm,
    send_ref,
    keep_ref,
    live_ref,
    poles_ref,
    roots_ref,
    slab_ref,
    map_ref,
    coupling_ref,
    deflated_ref,
    sems,
    *,
    groups,
    cols_dev,
):
    moves = [
        pltpu.make_async_copy(src, dst, sems.at[k])
        for k, (src, dst) in enumerate(
            (
                (map_hbm, map_ref),
                (coupling_hbm, coupling_ref),
                (deflated_hbm, deflated_ref),
                (poles_hbm, poles_ref),
                (roots_hbm, roots_ref),
                (slab_hbm, slab_ref),
            )
        )
    ]
    for move in moves:
        move.start()
    for move in moves[:4]:
        move.wait()
    chunks = map_ref.shape[0]
    rows_dev = cols_dev // LANES
    total = groups * rows_dev
    within = map_ref[...] - half_ref[0] * (groups * cols_dev)
    valid = (within >= 0) & (within < groups * cols_dev)
    target = (within >> log2(cols_dev)) & (groups - 1)
    place = bit_reverse(target ^ me_ref[0], log2(groups))
    row = place * rows_dev + ((within >> log2(LANES)) & (rows_dev - 1))
    row = jnp.where(valid, row, -1)
    lane = within & (LANES - 1)
    live = jnp.where(deflated_ref[...] == 0, coupling_ref[...], 0.0)
    live_ref[...] = live
    pieces = [p.astype(F32) for p in pieces_of(live, 3) + pieces_of(poles_ref[...], 3)]
    row_ids = lax.broadcasted_iota(jnp.int32, (total, LANES), 0)
    lane_ids = lax.broadcasted_iota(jnp.int32, (LANES, LANES), 0)
    left = [[] for _ in pieces]
    right = []
    for c in range(chunks):
        hit = row_ids == row[c : c + 1]
        for k, piece in enumerate(pieces):
            left[k].append(jnp.where(hit, piece[c : c + 1], 0.0).astype(BF16))
        right.append(jnp.where(lane_ids == lane[c : c + 1], 1.0, 0.0).astype(BF16))
    right = jnp.concatenate(right, axis=1)
    left = jnp.concatenate([jnp.concatenate(part, axis=1) for part in left], axis=0)
    dense = lax.dot_general(left, right, NT, preferred_element_type=F32).reshape(6, total, LANES)
    z = (dense[0] + dense[1] + dense[2]).reshape(2, groups // 2, rows_dev, LANES)
    d = (dense[3] + dense[4] + dense[5]).reshape(2, groups // 2, rows_dev, LANES)
    keep_ref[:, :rows_dev, :] = z[0]
    keep_ref[:, rows_dev:, :] = d[0]
    send_ref[:, :rows_dev, :] = z[1]
    send_ref[:, rows_dev:, :] = d[1]
    for move in moves[4:]:
        move.wait()


def split_kernel(slab_ref, hi_ref, lo_ref):
    slab = slab_ref[...]
    hi = slab.astype(BF16)
    hi_ref[...] = hi
    lo_ref[...] = (slab - hi.astype(F32)).astype(BF16)


def squares_kernel(roots_ref, live_ref, poles_ref, squares_ref):
    window = roots_ref.shape[1]
    roots_t = jnp.broadcast_to(roots_ref[...], (LANES, window)).T
    live = live_ref[...]
    poles = poles_ref[...]
    total = jnp.zeros((window, LANES), F32)
    for c in range(live.shape[0]):
        entry = live[c : c + 1] / (poles[c : c + 1] - roots_t)
        total = total + entry * entry
    squares_ref[...] = jnp.broadcast_to(jnp.sum(total.T, axis=0, keepdims=True), squares_ref.shape)


def product_kernel(me_ref, zd_ref, roots_ref, hi_ref, lo_ref, send_ref, keep_ref, *, groups):
    rows_dev = zd_ref.shape[0] // 2
    window = roots_ref.shape[1]
    zd = zd_ref[...].T
    parts = []
    for c in range(rows_dev):
        parts.append(zd[:, c : c + 1] / (zd[:, rows_dev + c : rows_dev + c + 1] - roots_ref[...]))
    factor = jnp.concatenate(pieces_of(jnp.concatenate(parts, axis=0), 2), axis=1)
    block = hi_ref.shape[0] // groups
    for ref, lead in ((send_ref, 1), (keep_ref, 0)):
        left = [[], []]
        for m in range(groups // 2):
            place = lead * (groups // 2) + m
            rel = int(format(place, f"0{log2(groups)}b")[::-1], 2)
            start = pl.multiple_of((me_ref[0] ^ rel) * block, block)
            left[0].append(hi_ref[pl.ds(start, block), :])
            left[1].append(lo_ref[pl.ds(start, block), :])
        left = jnp.concatenate(left[0] + left[1], axis=0)
        out = jnp.dot(left, factor, preferred_element_type=F32)
        half = out.shape[0] // 2
        out = out[:half] + out[half:]
        ref[...] = out[:, :window] + out[:, window:]


def exchange(value, groups, bit):
    return lax.ppermute(value, "col", [(i, i ^ bit) for i in range(groups)])


def body(eigen_slab, secular_poles, coupling, window_roots, deflated, column_map):
    groups = lax.axis_size("col")
    row_groups = lax.axis_size("row")
    rows, cols_dev = eigen_slab.shape
    window = window_roots.shape[0]
    bits = log2(groups)
    half = (lax.axis_index("row") >= row_groups // 2).astype(jnp.int32).reshape(1)
    me = lax.axis_index("col").astype(jnp.int32).reshape(1)
    tiled = lambda a: a.reshape(-1, LANES)
    rows_dev = cols_dev // LANES
    smem = pl.BlockSpec(memory_space=pltpu.SMEM)
    vmem = pl.BlockSpec(memory_space=pltpu.VMEM)

    hbm = pl.BlockSpec(memory_space=pltpu.HBM)

    placed = pltpu.VMEM((groups // 2, 2 * rows_dev, LANES), F32)
    column_map, coupling, deflated, secular_poles = map(tiled, (column_map, coupling, deflated, secular_poles))
    listed = coupling.shape
    send, keep, live, poles, roots, slab = pl.pallas_call(
        functools.partial(place_kernel, groups=groups, cols_dev=cols_dev),
        out_shape=(
            placed,
            placed,
            pltpu.VMEM(listed, F32),
            pltpu.VMEM(listed, F32),
            pltpu.VMEM((1, window), F32),
            pltpu.VMEM((rows, cols_dev), F32),
        ),
        in_specs=[smem] * 2 + [hbm] * 6,
        out_specs=(vmem,) * 6,
        scratch_shapes=[
            pltpu.VMEM(listed, jnp.int32),
            pltpu.VMEM(listed, F32),
            pltpu.VMEM(listed, jnp.int32),
            pltpu.SemaphoreType.DMA((6,)),
        ],
        name="place",
        compiler_params=PARAMS,
    )(
        half,
        me,
        *(
            pltpu.with_memory_space_constraint(a, pltpu.HBM)
            for a in (column_map, coupling, deflated, secular_poles, window_roots.reshape(1, window), eigen_slab)
        ),
    )

    term = pltpu.VMEM((rows, cols_dev), BF16)
    hi, lo = pl.pallas_call(
        split_kernel,
        out_shape=(term, term),
        in_specs=[vmem],
        out_specs=(vmem, vmem),
        name="split_slab",
        compiler_params=PARAMS,
    )(slab)
    squares = pl.pallas_call(
        squares_kernel,
        out_shape=pltpu.VMEM((SUBLANES, window), F32),
        in_specs=[vmem] * 3,
        out_specs=vmem,
        name="sum_squares",
        compiler_params=PARAMS,
    )(roots, live, poles)

    value = keep + exchange(send, groups, 1)
    for b in range(1, bits):
        mid = value.shape[0] // 2
        value = value[:mid] + exchange(value[mid:], groups, 1 << b)

    half_rows = pltpu.VMEM((rows // 2, window), F32)
    send, keep = pl.pallas_call(
        functools.partial(product_kernel, groups=groups),
        out_shape=(half_rows, half_rows),
        in_specs=[smem, vmem, vmem, vmem, vmem],
        out_specs=(vmem, vmem),
        name="product",
        compiler_params=PARAMS,
    )(me, value.reshape(2 * rows_dev, LANES), roots, hi, lo)

    for b in range(bits):
        got = exchange(jnp.concatenate([send, squares]), groups, 1 << b)
        mid = send.shape[0]
        keep = keep + got[:mid]
        squares = squares + got[mid:]
        if b + 1 < bits:
            keep, send = keep[: mid // 2], keep[mid // 2 :]
    return keep * lax.rsqrt(squares[:1])


def solution(mesh):
    return jax.shard_map(
        body,
        mesh=mesh,
        in_specs=(P("row", "col"), P("col"), P("col"), P(), P("col"), P("col")),
        out_specs=P(("row", "col"), None),
        check_vma=False,
    )
```

```python
import functools

import jax
import jax.numpy as jnp
from jax import lax
from jax.experimental import pallas as pl
from jax.experimental.pallas import tpu as pltpu
from jax.sharding import PartitionSpec as P


LANES = 128
SUBLANES = 8
F32 = jnp.float32
BF16 = jnp.bfloat16
NT = (((1,), (1,)), ((), ()))
PARAMS = pltpu.CompilerParams(vmem_limit_bytes=24 * 2**20)


def log2(n):
    assert n > 0 and n & (n - 1) == 0
    return n.bit_length() - 1


def bit_reverse(value, bits):
    out = jnp.zeros_like(value)
    for b in range(bits):
        out = out | (((value >> b) & 1) << (bits - 1 - b))
    return out


def pieces_of(value, count):
    out = []
    for _ in range(count):
        piece = value.astype(BF16)
        out.append(piece)
        value = value - piece.astype(F32)
    return out


def place_kernel(
    half_ref,
    me_ref,
    map_hbm,
    coupling_hbm,
    deflated_hbm,
    poles_hbm,
    roots_hbm,
    slab_hbm,
    dense_ref,
    live_ref,
    poles_ref,
    roots_ref,
    slab_ref,
    map_ref,
    coupling_ref,
    deflated_ref,
    sems,
    *,
    groups,
    cols_dev,
):
    moves = [
        pltpu.make_async_copy(src, dst, sems.at[k])
        for k, (src, dst) in enumerate(
            (
                (map_hbm, map_ref),
                (coupling_hbm, coupling_ref),
                (deflated_hbm, deflated_ref),
                (poles_hbm, poles_ref),
                (roots_hbm, roots_ref),
                (slab_hbm, slab_ref),
            )
        )
    ]
    for move in moves:
        move.start()
    for move in moves[:4]:
        move.wait()
    chunks = map_ref.shape[0]
    rows_dev = cols_dev // LANES
    total = groups * rows_dev
    within = map_ref[...] - half_ref[0] * (groups * cols_dev)
    valid = (within >= 0) & (within < groups * cols_dev)
    target = (within >> log2(cols_dev)) & (groups - 1)
    place = bit_reverse((target ^ me_ref[0]) >> 1, log2(groups) - 1) * 2 + (target & 1)
    row = place * rows_dev + ((within >> log2(LANES)) & (rows_dev - 1))
    row = jnp.where(valid, row, -1)
    lane = within & (LANES - 1)
    live = jnp.where(deflated_ref[...] == 0, coupling_ref[...], 0.0)
    live_ref[...] = live
    pieces = [p.astype(F32) for p in pieces_of(live, 3) + pieces_of(poles_ref[...], 3)]
    row_ids = lax.broadcasted_iota(jnp.int32, (total, LANES), 0)
    lane_ids = lax.broadcasted_iota(jnp.int32, (LANES, LANES), 0)
    left = [[] for _ in pieces]
    right = []
    for c in range(chunks):
        hit = row_ids == row[c : c + 1]
        for k, piece in enumerate(pieces):
            left[k].append(jnp.where(hit, piece[c : c + 1], 0.0).astype(BF16))
        right.append(jnp.where(lane_ids == lane[c : c + 1], 1.0, 0.0).astype(BF16))
    right = jnp.concatenate(right, axis=1)
    left = jnp.concatenate([jnp.concatenate(part, axis=1) for part in left], axis=0)
    dense = lax.dot_general(left, right, NT, preferred_element_type=F32).reshape(6, total, LANES)
    dense_ref[:, :rows_dev, :] = (dense[0] + dense[1] + dense[2]).reshape(groups, rows_dev, LANES)
    dense_ref[:, rows_dev:, :] = (dense[3] + dense[4] + dense[5]).reshape(groups, rows_dev, LANES)
    for move in moves[4:]:
        move.wait()


def split_kernel(slab_ref, hi_ref, lo_ref):
    slab = slab_ref[...]
    hi = slab.astype(BF16)
    hi_ref[...] = hi
    lo_ref[...] = (slab - hi.astype(F32)).astype(BF16)


def squares_kernel(roots_ref, live_ref, poles_ref, squares_ref):
    window = roots_ref.shape[1]
    roots_t = jnp.broadcast_to(roots_ref[...], (LANES, window)).T
    live = live_ref[...]
    poles = poles_ref[...]
    total = jnp.zeros((window, LANES), F32)
    for c in range(live.shape[0]):
        entry = live[c : c + 1] / (poles[c : c + 1] - roots_t)
        total = total + entry * entry
    squares_ref[...] = jnp.broadcast_to(jnp.sum(total.T, axis=0, keepdims=True), squares_ref.shape)


def rows_of(refs, me_ref, lead, chips):
    block = refs[0].shape[0] // chips
    out = []
    for m in range(chips // 2):
        place = lead * (chips // 2) + m
        rel = int(format(place, f"0{log2(chips)}b")[::-1], 2)
        start = pl.multiple_of(((me_ref[0] >> 1) ^ rel) * block, block)
        out.append(jnp.concatenate([ref[pl.ds(start, block), :] for ref in refs], axis=1))
    return out


def half_product(me_ref, factor, hi0_ref, lo0_ref, hi1_ref, lo1_ref, lead, chips):
    left = rows_of((hi0_ref, hi1_ref), me_ref, lead, chips) + rows_of((lo0_ref, lo1_ref), me_ref, lead, chips)
    out = jnp.dot(jnp.concatenate(left, axis=0), factor, preferred_element_type=F32)
    half = out.shape[0] // 2
    window = out.shape[1] // 2
    out = out[:half] + out[half:]
    return out[:, :window] + out[:, window:]


def send_kernel(
    me_ref, zd_ref, roots_ref, squares_ref, hi0_ref, lo0_ref, hi1_ref, lo1_ref, send_ref, factor_ref, *, chips
):
    rows_dev = zd_ref.shape[0] // 4
    zd = zd_ref[...].T
    parts = []
    for c in range(2 * rows_dev):
        k = c + (c // rows_dev) * rows_dev
        parts.append(zd[:, k : k + 1] / (zd[:, rows_dev + k : rows_dev + k + 1] - roots_ref[...]))
    factor = jnp.concatenate(pieces_of(jnp.concatenate(parts, axis=0), 2), axis=1)
    factor_ref[...] = factor
    half = hi0_ref.shape[0] // 2
    send_ref[:half] = half_product(me_ref, factor, hi0_ref, lo0_ref, hi1_ref, lo1_ref, 1, chips)
    send_ref[half:] = squares_ref[...]


def keep_kernel(me_ref, factor_ref, hi0_ref, lo0_ref, hi1_ref, lo1_ref, keep_ref, *, chips):
    keep_ref[...] = half_product(me_ref, factor_ref[...], hi0_ref, lo0_ref, hi1_ref, lo1_ref, 0, chips)


def permute(value, pairs):
    return lax.ppermute(value, "col", pairs)


def body(eigen_slab, secular_poles, coupling, window_roots, deflated, column_map):
    groups = lax.axis_size("col")
    row_groups = lax.axis_size("row")
    rows, cols_dev = eigen_slab.shape
    window = window_roots.shape[0]
    bits = log2(groups)
    chips = groups // 2
    half = (lax.axis_index("row") >= row_groups // 2).astype(jnp.int32).reshape(1)
    me = lax.axis_index("col").astype(jnp.int32).reshape(1)
    tiled = lambda a: a.reshape(-1, LANES)
    rows_dev = cols_dev // LANES
    smem = pl.BlockSpec(memory_space=pltpu.SMEM)
    vmem = pl.BlockSpec(memory_space=pltpu.VMEM)
    hbm = pl.BlockSpec(memory_space=pltpu.HBM)
    up = [(i, i + 1) for i in range(0, groups, 2)]
    down = [(i + 1, i) for i in range(0, groups, 2)]
    across = [[(i, i ^ (1 << b)) for i in range(1, groups, 2)] for b in range(1, bits)]

    column_map, coupling, deflated, secular_poles = map(tiled, (column_map, coupling, deflated, secular_poles))
    listed = coupling.shape
    dense, live, poles, roots, slab = pl.pallas_call(
        functools.partial(place_kernel, groups=groups, cols_dev=cols_dev),
        out_shape=(
            pltpu.VMEM((groups, 2 * rows_dev, LANES), F32),
            pltpu.VMEM(listed, F32),
            pltpu.VMEM(listed, F32),
            pltpu.VMEM((1, window), F32),
            pltpu.VMEM((rows, cols_dev), F32),
        ),
        in_specs=[smem] * 2 + [hbm] * 6,
        out_specs=(vmem,) * 5,
        scratch_shapes=[
            pltpu.VMEM(listed, jnp.int32),
            pltpu.VMEM(listed, F32),
            pltpu.VMEM(listed, jnp.int32),
            pltpu.SemaphoreType.DMA((6,)),
        ],
        name="place",
        compiler_params=PARAMS,
    )(
        half,
        me,
        *(
            pltpu.with_memory_space_constraint(a, pltpu.HBM)
            for a in (column_map, coupling, deflated, secular_poles, window_roots.reshape(1, window), eigen_slab)
        ),
    )

    def split(slab):
        term = pltpu.VMEM((rows, cols_dev), BF16)
        return pl.pallas_call(
            split_kernel,
            out_shape=(term, term),
            in_specs=[vmem],
            out_specs=(vmem, vmem),
            name="split_slab",
            compiler_params=PARAMS,
        )(slab)

    squares = pl.pallas_call(
        squares_kernel,
        out_shape=pltpu.VMEM((SUBLANES, window), F32),
        in_specs=[vmem] * 3,
        out_specs=vmem,
        name="sum_squares",
        compiler_params=PARAMS,
    )(roots, live, poles)

    value = dense + permute(dense, up)
    slab0 = permute(slab, up)
    squares = squares + permute(squares, up)
    for b, pairs in enumerate(across, 1):
        mid = value.shape[0] // 2
        value = value[:mid] + permute(value[mid:], pairs)

    terms = (*split(slab0), *split(slab))
    send, factor = pl.pallas_call(
        functools.partial(send_kernel, chips=chips),
        out_shape=(
            pltpu.VMEM((rows // 2 + SUBLANES, window), F32),
            pltpu.VMEM((2 * cols_dev, 2 * window), BF16),
        ),
        in_specs=[smem] + [vmem] * 7,
        out_specs=(vmem, vmem),
        name="send_rows",
        compiler_params=PARAMS,
    )(me, value.reshape(4 * rows_dev, LANES), roots, squares, *terms)
    keep = pl.pallas_call(
        functools.partial(keep_kernel, chips=chips),
        out_shape=pltpu.VMEM((rows // 2, window), F32),
        in_specs=[smem] + [vmem] * 5,
        out_specs=vmem,
        name="keep_rows",
        compiler_params=PARAMS,
    )(me, factor, *terms)

    for b, pairs in enumerate(across, 1):
        got = permute(send, pairs)
        mid = keep.shape[0]
        keep = keep + got[:mid]
        squares = squares + got[mid:]
        if b + 1 < bits:
            keep, send = keep[: mid // 2], jnp.concatenate([keep[mid // 2 :], squares])
    mid = keep.shape[0] // 2
    got = permute(jnp.concatenate([keep[:mid], squares]), down)
    mine = (me & 1) == 1
    return jnp.where(mine, keep[mid:], got[:mid]) * lax.rsqrt(jnp.where(mine, squares[:1], got[mid : mid + 1]))


def solution(mesh):
    return jax.shard_map(
        body,
        mesh=mesh,
        in_specs=(P("row", "col"), P("col"), P("col"), P(), P("col"), P("col")),
        out_specs=P(("row", "col"), None),
        check_vma=False,
    )
```

```python
import functools

import jax
import jax.numpy as jnp
from jax import lax
from jax.experimental import pallas as pl
from jax.experimental.pallas import tpu as pltpu
from jax.sharding import PartitionSpec as P


LANES = 128
SUBLANES = 8
F32 = jnp.float32
BF16 = jnp.bfloat16
NT = (((1,), (1,)), ((), ()))
PARAMS = pltpu.CompilerParams(vmem_limit_bytes=24 * 2**20)


def log2(n):
    assert n > 0 and n & (n - 1) == 0
    return n.bit_length() - 1


def parity(value):
    return bin(value).count("1") & 1


def stage_bits(bits, role):
    order = list(range(bits))
    if role and bits > 1:
        order[0], order[1] = 1, 0
    return order


def role_of(device, bits):
    return (device ^ (device >> 1) ^ (device >> 2)) & 1 if bits > 1 else device * 0


def partner(device, stage, bits):
    return device ^ ((2 << stage_bits(bits, role_of(device, bits))[stage]) | 1)


def relative_at(place, bits, role):
    return sum(((place >> (bits - 1 - s)) & 1) << bit for s, bit in enumerate(stage_bits(bits, role)))


def place_of(relative, bits, role):
    if bits > 1:
        unequal = (relative ^ (relative >> 1)) & role
        relative = relative ^ (unequal | (unequal << 1))
    out = jnp.zeros_like(relative)
    for b in range(bits):
        out = out | (((relative >> b) & 1) << (bits - 1 - b))
    return out


def other_role_place(place, bits):
    return next(p for p in range(1 << bits) if relative_at(p, bits, 1) == relative_at(place, bits, 0))


def owner_at(device, place, bits, role):
    masks = [(r << 1) | parity(r) for r in (relative_at(place, bits, 0), relative_at(place, bits, 1))]
    return device ^ jnp.where(role == 0, masks[0], masks[1])


def pieces_of(value, count):
    out = []
    for _ in range(count):
        piece = value.astype(BF16)
        out.append(piece)
        value = value - piece.astype(F32)
    return out


def place_kernel(
    half_ref,
    me_ref,
    map_hbm,
    coupling_hbm,
    deflated_hbm,
    poles_hbm,
    roots_hbm,
    slab_hbm,
    give_ref,
    dense_ref,
    live_ref,
    poles_ref,
    roots_ref,
    slab_give_ref,
    slab_ref,
    map_ref,
    coupling_ref,
    deflated_ref,
    sems,
    *,
    groups,
    cols_dev,
):
    bits = log2(groups) - 1
    me = me_ref[0]
    role = role_of(me, bits)
    moves = [
        (map_hbm, map_ref),
        (coupling_hbm, coupling_ref),
        (deflated_hbm, deflated_ref),
        (poles_hbm, poles_ref),
        (roots_hbm, roots_ref),
    ]
    block = slab_hbm.shape[0] // groups
    for ref, device, order in ((slab_give_ref, me ^ 1, 1 - role if bits > 1 else role), (slab_ref, me, role)):
        for p in range(groups // 2):
            start = pl.multiple_of(owner_at(device, p, bits, order) * block, block)
            moves.append((slab_hbm.at[pl.ds(start, block), :], ref.at[p * block : (p + 1) * block, :]))
    moves = [pltpu.make_async_copy(src, dst, sems.at[k]) for k, (src, dst) in enumerate(moves)]
    for move in moves:
        move.start()
    for move in moves[:4]:
        move.wait()
    chunks = map_ref.shape[0]
    rows_dev = cols_dev // LANES
    total = groups * rows_dev
    within = map_ref[...] - half_ref[0] * (groups * cols_dev)
    valid = (within >= 0) & (within < groups * cols_dev)
    target = (within >> log2(cols_dev)) & (groups - 1)
    place = place_of((target ^ me) >> 1, bits, role) * 2 + (target & 1)
    row = place * rows_dev + ((within >> log2(LANES)) & (rows_dev - 1))
    row = jnp.where(valid, row, -1)
    lane = within & (LANES - 1)
    live = jnp.where(deflated_ref[...] == 0, coupling_ref[...], 0.0)
    live_ref[...] = live
    pieces = [p.astype(F32) for p in pieces_of(live, 3) + pieces_of(poles_ref[...], 3)]
    row_ids = lax.broadcasted_iota(jnp.int32, (total, LANES), 0)
    lane_ids = lax.broadcasted_iota(jnp.int32, (LANES, LANES), 0)
    left = [[] for _ in pieces]
    right = []
    for c in range(chunks):
        hit = row_ids == row[c : c + 1]
        for k, piece in enumerate(pieces):
            left[k].append(jnp.where(hit, piece[c : c + 1], 0.0).astype(BF16))
        right.append(jnp.where(lane_ids == lane[c : c + 1], 1.0, 0.0).astype(BF16))
    right = jnp.concatenate(right, axis=1)
    left = jnp.concatenate([jnp.concatenate(part, axis=1) for part in left], axis=0)
    dense = lax.dot_general(left, right, NT, preferred_element_type=F32).reshape(6, total, LANES)
    field = 2 * rows_dev
    both = (dense[0] + dense[1] + dense[2], dense[3] + dense[4] + dense[5])
    for k, value in enumerate(both):
        value = value.reshape(groups // 2, field, LANES)
        dense_ref[:, k * field : (k + 1) * field, :] = value
        for p in range(groups // 2):
            give_ref[p, k * field : (k + 1) * field, :] = value[other_role_place(p, bits)]
    for move in moves[4:]:
        move.wait()


def split_kernel(slab_ref, hi_ref, lo_ref):
    slab = slab_ref[...]
    hi = slab.astype(BF16)
    hi_ref[...] = hi
    lo_ref[...] = (slab - hi.astype(F32)).astype(BF16)


def squares_kernel(roots_ref, live_ref, poles_ref, squares_ref):
    window = roots_ref.shape[1]
    roots_t = jnp.broadcast_to(roots_ref[...], (LANES, window)).T
    live = live_ref[...]
    poles = poles_ref[...]
    total = jnp.zeros((window, LANES), F32)
    for c in range(live.shape[0]):
        entry = live[c : c + 1] / (poles[c : c + 1] - roots_t)
        total = total + entry * entry
    squares_ref[...] = jnp.broadcast_to(jnp.sum(total.T, axis=0, keepdims=True), squares_ref.shape)


def half_product(factor, hi0_ref, lo0_ref, hi1_ref, lo1_ref, lead):
    rows = hi0_ref.shape[0] // 2
    rows = slice(lead * rows, (lead + 1) * rows)
    hi = jnp.concatenate([hi0_ref[rows, :], hi1_ref[rows, :]], axis=1)
    lo = jnp.concatenate([lo0_ref[rows, :], lo1_ref[rows, :]], axis=1)
    out = jnp.dot(jnp.concatenate([hi, lo], axis=0), factor, preferred_element_type=F32)
    half = out.shape[0] // 2
    window = out.shape[1] // 2
    out = out[:half] + out[half:]
    return out[:, :window] + out[:, window:]


def send_kernel(me_ref, zd_ref, roots_ref, squares_ref, hi0_ref, lo0_ref, hi1_ref, lo1_ref, send_ref, factor_ref):
    rows_dev = zd_ref.shape[0] // 4
    core = me_ref[0] & 1
    own = pl.multiple_of(core * rows_dev, rows_dev)
    other = pl.multiple_of((1 - core) * rows_dev, rows_dev)
    field = 2 * rows_dev
    zd = jnp.concatenate([zd_ref[pl.ds(k + at, rows_dev), :] for k in (0, field) for at in (own, other)], axis=0).T
    parts = []
    for c in range(field):
        parts.append(zd[:, c : c + 1] / (zd[:, field + c : field + c + 1] - roots_ref[...]))
    factor = jnp.concatenate(pieces_of(jnp.concatenate(parts, axis=0), 2), axis=1)
    factor_ref[...] = factor
    half = hi0_ref.shape[0] // 2
    send_ref[:half] = half_product(factor, hi0_ref, lo0_ref, hi1_ref, lo1_ref, 1)
    send_ref[half:] = squares_ref[...]


def keep_kernel(factor_ref, hi0_ref, lo0_ref, hi1_ref, lo1_ref, keep_ref):
    keep_ref[...] = half_product(factor_ref[...], hi0_ref, lo0_ref, hi1_ref, lo1_ref, 0)


def permute(value, pairs):
    return lax.ppermute(value, "col", pairs)


def body(eigen_slab, secular_poles, coupling, window_roots, deflated, column_map):
    groups = lax.axis_size("col")
    row_groups = lax.axis_size("row")
    rows, cols_dev = eigen_slab.shape
    window = window_roots.shape[0]
    bits = log2(groups) - 1
    half = (lax.axis_index("row") >= row_groups // 2).astype(jnp.int32).reshape(1)
    me = lax.axis_index("col").astype(jnp.int32).reshape(1)
    tiled = lambda a: a.reshape(-1, LANES)
    rows_dev = cols_dev // LANES
    smem = pl.BlockSpec(memory_space=pltpu.SMEM)
    vmem = pl.BlockSpec(memory_space=pltpu.VMEM)
    hbm = pl.BlockSpec(memory_space=pltpu.HBM)
    mate = [(i, i ^ 1) for i in range(groups)]
    across = [[(i, partner(i, stage, bits)) for i in range(groups)] for stage in range(bits)]

    column_map, coupling, deflated, secular_poles = map(tiled, (column_map, coupling, deflated, secular_poles))
    listed = coupling.shape
    give, dense, live, poles, roots, slab_give, slab = pl.pallas_call(
        functools.partial(place_kernel, groups=groups, cols_dev=cols_dev),
        out_shape=(
            pltpu.VMEM((groups // 2, 4 * rows_dev, LANES), F32),
            pltpu.VMEM((groups // 2, 4 * rows_dev, LANES), F32),
            pltpu.VMEM(listed, F32),
            pltpu.VMEM(listed, F32),
            pltpu.VMEM((1, window), F32),
            pltpu.VMEM((rows // 2, cols_dev), F32),
            pltpu.VMEM((rows // 2, cols_dev), F32),
        ),
        in_specs=[smem] * 2 + [hbm] * 6,
        out_specs=(vmem,) * 7,
        scratch_shapes=[
            pltpu.VMEM(listed, jnp.int32),
            pltpu.VMEM(listed, F32),
            pltpu.VMEM(listed, jnp.int32),
            pltpu.SemaphoreType.DMA((5 + groups,)),
        ],
        name="place",
        compiler_params=PARAMS,
    )(
        half,
        me,
        *(
            pltpu.with_memory_space_constraint(a, pltpu.HBM)
            for a in (column_map, coupling, deflated, secular_poles, window_roots.reshape(1, window), eigen_slab)
        ),
    )

    def split(slab):
        term = pltpu.VMEM((rows // 2, cols_dev), BF16)
        return pl.pallas_call(
            split_kernel,
            out_shape=(term, term),
            in_specs=[vmem],
            out_specs=(vmem, vmem),
            name="split_slab",
            compiler_params=PARAMS,
        )(slab)

    squares = pl.pallas_call(
        squares_kernel,
        out_shape=pltpu.VMEM((SUBLANES, window), F32),
        in_specs=[vmem] * 3,
        out_specs=vmem,
        name="sum_squares",
        compiler_params=PARAMS,
    )(roots, live, poles)

    value = dense + permute(give, mate)
    slab_got = permute(slab_give, mate)
    squares = squares + permute(squares, mate)
    for stage, pairs in enumerate(across, 1):
        mid = value.shape[0] // 2
        value = value[:mid] + permute(value[mid:], pairs)

    terms = (*split(slab), *split(slab_got))
    send, factor = pl.pallas_call(
        send_kernel,
        out_shape=(
            pltpu.VMEM((rows // 4 + SUBLANES, window), F32),
            pltpu.VMEM((2 * cols_dev, 2 * window), BF16),
        ),
        in_specs=[smem] + [vmem] * 7,
        out_specs=(vmem, vmem),
        name="send_rows",
        compiler_params=PARAMS,
    )(me, value.reshape(4 * rows_dev, LANES), roots, squares, *terms)
    keep = pl.pallas_call(
        keep_kernel,
        out_shape=pltpu.VMEM((rows // 4, window), F32),
        in_specs=[vmem] * 5,
        out_specs=vmem,
        name="keep_rows",
        compiler_params=PARAMS,
    )(factor, *terms)

    for stage, pairs in enumerate(across, 1):
        got = permute(send, pairs)
        mid = keep.shape[0]
        keep = keep + got[:mid]
        squares = squares + got[mid:]
        if stage < bits:
            keep, send = keep[: mid // 2], jnp.concatenate([keep[mid // 2 :], squares])
    return keep * lax.rsqrt(squares[:1])


def solution(mesh):
    return jax.shard_map(
        body,
        mesh=mesh,
        in_specs=(P("row", "col"), P("col"), P("col"), P(), P("col"), P("col")),
        out_specs=P(("row", "col"), None),
        check_vma=False,
    )
```

```python
import functools

import jax
import jax.numpy as jnp
from jax import lax
from jax.experimental import pallas as pl
from jax.experimental.pallas import tpu as pltpu
from jax.sharding import PartitionSpec as P


LANES = 128
SUBLANES = 8
F32 = jnp.float32
BF16 = jnp.bfloat16
NT = (((1,), (1,)), ((), ()))
PARAMS = pltpu.CompilerParams(vmem_limit_bytes=24 * 2**20)


def log2(n):
    assert n > 0 and n & (n - 1) == 0
    return n.bit_length() - 1


def parity(value):
    return bin(value).count("1") & 1


def stage_bits(bits, role):
    order = list(range(bits))
    if role and bits > 1:
        order[0], order[1] = 1, 0
    return order


def role_of(device, bits):
    return (device ^ (device >> 1) ^ (device >> 2)) & 1 if bits > 1 else device * 0


def partner(device, stage, bits):
    return device ^ ((2 << stage_bits(bits, role_of(device, bits))[stage]) | 1)


def relative_at(place, bits, role):
    return sum(((place >> (bits - 1 - s)) & 1) << bit for s, bit in enumerate(stage_bits(bits, role)))


def place_of(relative, bits, role):
    if bits > 1:
        unequal = (relative ^ (relative >> 1)) & role
        relative = relative ^ (unequal | (unequal << 1))
    out = jnp.zeros_like(relative)
    for b in range(bits):
        out = out | (((relative >> b) & 1) << (bits - 1 - b))
    return out


def other_role_place(place, bits):
    return next(p for p in range(1 << bits) if relative_at(p, bits, 1) == relative_at(place, bits, 0))


def owner_at(device, place, bits, role):
    masks = [(r << 1) | parity(r) for r in (relative_at(place, bits, 0), relative_at(place, bits, 1))]
    return device ^ jnp.where(role == 0, masks[0], masks[1])


def pieces_of(value, count):
    out = []
    for _ in range(count):
        piece = value.astype(BF16)
        out.append(piece)
        value = value - piece.astype(F32)
    return out


def slab_moves(slab_hbm, slab_ref, device, bits):
    chips = 1 << bits
    block = slab_ref.shape[0] // chips
    moves = []
    for p in range(chips):
        start = pl.multiple_of(owner_at(device, p, bits, role_of(device, bits)) * block, block)
        moves.append((slab_hbm.at[pl.ds(start, block), :], slab_ref.at[p * block : (p + 1) * block, :]))
    return moves


def place_kernel(
    half_ref,
    me_ref,
    map_hbm,
    coupling_hbm,
    deflated_hbm,
    poles_hbm,
    roots_hbm,
    slab_hbm,
    give_ref,
    dense_ref,
    live_ref,
    poles_ref,
    roots_ref,
    slab_give_ref,
    map_ref,
    coupling_ref,
    deflated_ref,
    sems,
    *,
    groups,
    cols_dev,
):
    bits = log2(groups) - 1
    me = me_ref[0]
    role = role_of(me, bits)
    moves = [
        (map_hbm, map_ref),
        (coupling_hbm, coupling_ref),
        (deflated_hbm, deflated_ref),
        (poles_hbm, poles_ref),
        (roots_hbm, roots_ref),
    ]
    moves += slab_moves(slab_hbm, slab_give_ref, me ^ 1, bits)
    moves = [pltpu.make_async_copy(src, dst, sems.at[k]) for k, (src, dst) in enumerate(moves)]
    for move in moves:
        move.start()
    for move in moves[:4]:
        move.wait()
    chunks = map_ref.shape[0]
    wide = 2 * LANES
    rows_dev = cols_dev // wide
    total = groups * rows_dev
    within = map_ref[...] - half_ref[0] * (groups * cols_dev)
    valid = (within >= 0) & (within < groups * cols_dev)
    target = (within >> log2(cols_dev)) & (groups - 1)
    place = place_of((target ^ me) >> 1, bits, role) * 2 + (target & 1)
    row = place * rows_dev + ((within >> log2(wide)) & (rows_dev - 1))
    row = jnp.where(valid, row, -1)
    lane = within & (wide - 1)
    live = jnp.where(deflated_ref[...] == 0, coupling_ref[...], 0.0)
    live_ref[...] = live
    pieces = [p.astype(F32) for p in pieces_of(live, 3) + pieces_of(poles_ref[...], 3)]
    group = 2 * SUBLANES
    ids = lax.broadcasted_iota(jnp.int32, (group, LANES), 0).astype(F32)
    packed = lambda value, c: jnp.broadcast_to(value[c : c + 1], (group, LANES)).astype(BF16)
    row, lane = row.astype(F32), lane.astype(F32)
    left = [[] for _ in pieces]
    right = []
    zero, one = jnp.zeros((group, LANES), BF16), jnp.ones((group, LANES), BF16)
    for c in range(chunks):
        row_c, lane_c = packed(row, c), packed(lane, c)
        hits = [row_c == (ids + g).astype(BF16) for g in range(0, total, group)]
        for k, piece in enumerate(pieces):
            piece_c = packed(piece, c)
            left[k].append(jnp.concatenate([jnp.where(hit, piece_c, zero) for hit in hits], axis=0))
        right.append(
            jnp.concatenate([jnp.where(lane_c == (ids + g).astype(BF16), one, zero) for g in range(0, wide, group)], axis=0)
        )
    right = jnp.concatenate(right, axis=1)
    left = jnp.concatenate([jnp.concatenate(part, axis=1) for part in left], axis=0)
    dense = lax.dot_general(left, right, NT, preferred_element_type=F32).reshape(6, groups // 2, 2 * rows_dev, wide)
    both = (dense[0] + dense[1] + dense[2], dense[3] + dense[4] + dense[5])
    tile = 2 * rows_dev
    for k, value in enumerate(value[:, :, at : at + LANES] for value in both for at in (0, LANES)):
        rows = slice(k * tile, (k + 1) * tile)
        dense_ref[:, rows, :] = value
        for p in range(groups // 2):
            give_ref[p, rows, :] = value[other_role_place(p, bits)]
    for move in moves[4:]:
        move.wait()


def split(slab, hi_ref, lo_ref, rows):
    hi = slab.astype(BF16)
    hi_ref[rows, :] = hi
    lo_ref[rows, :] = (slab - hi.astype(F32)).astype(BF16)


def split_kernel(slab_ref, hi_ref, lo_ref):
    split(slab_ref[...], hi_ref, lo_ref, slice(None))


def fetch_split_kernel(me_ref, slab_hbm, hi_ref, lo_ref, slab_ref, sems, *, bits):
    moves = slab_moves(slab_hbm, slab_ref, me_ref[0], bits)
    moves = [pltpu.make_async_copy(src, dst, sems.at[k]) for k, (src, dst) in enumerate(moves)]
    for move in moves:
        move.start()
    block = slab_ref.shape[0] // len(moves)
    for k, move in enumerate(moves):
        move.wait()
        rows = slice(k * block, (k + 1) * block)
        split(slab_ref[rows, :], hi_ref, lo_ref, rows)


def squares_kernel(roots_ref, live_ref, poles_ref, squares_ref, roots_t_ref):
    window = roots_ref.shape[1]
    roots_t = jnp.broadcast_to(roots_ref[...], (LANES, window)).T
    roots_t_ref[...] = roots_t
    live = live_ref[...]
    poles = poles_ref[...]
    total = jnp.zeros((window, LANES), F32)
    for c in range(live.shape[0]):
        entry = live[c : c + 1] / (poles[c : c + 1] - roots_t)
        total = total + entry * entry
    squares_ref[...] = jnp.broadcast_to(jnp.sum(total.T, axis=0, keepdims=True), squares_ref.shape)


def half_product(factor_of, refs, lead):
    hi0_ref, lo0_ref, hi1_ref, lo1_ref = refs
    half = hi0_ref.shape[0] // 2
    rows = slice(lead * half, (lead + 1) * half)
    out = None
    for part, (hi_ref, lo_ref) in enumerate(((hi0_ref, lo0_ref), (hi1_ref, lo1_ref))):
        for step in range(hi_ref.shape[1] // (2 * LANES)):
            columns = slice(step * 2 * LANES, (step + 1) * 2 * LANES)
            left = jnp.concatenate([hi_ref[rows, columns], lo_ref[rows, columns]], axis=0)
            term = lax.dot_general(left, factor_of(part, step), NT, preferred_element_type=F32)
            out = term if out is None else out + term
    out = out[:half] + out[half:]
    window = out.shape[1] // 2
    return out[:, :window] + out[:, window:]


def send_kernel(me_ref, zd_ref, roots_t_ref, squares_ref, *refs):
    terms, (send_ref, factor_ref) = refs[:4], refs[4:]
    tile = zd_ref.shape[0] // 4
    rows_dev = tile // 2
    core = me_ref[0] & 1
    roots_t = roots_t_ref[...]

    def factor_of(part, step):
        row = (core if part == 0 else 1 - core) * rows_dev + step
        entries = [
            zd_ref[pl.ds(row + at, 1), :] / (zd_ref[pl.ds(row + at + 2 * tile, 1), :] - roots_t) for at in (0, tile)
        ]
        factor = jnp.concatenate(pieces_of(jnp.concatenate(entries, axis=1), 2), axis=0)
        at = (part * rows_dev + step) * 2 * LANES
        factor_ref[:, at : at + 2 * LANES] = factor
        return factor

    half = terms[0].shape[0] // 2
    send_ref[:half] = half_product(factor_of, terms, 1)
    send_ref[half:] = squares_ref[...]


def keep_kernel(factor_ref, *refs):
    terms, keep_ref = refs[:4], refs[4]
    steps = factor_ref.shape[1] // (4 * LANES)

    def factor_of(part, step):
        at = (part * steps + step) * 2 * LANES
        return factor_ref[:, at : at + 2 * LANES]

    keep_ref[...] = half_product(factor_of, terms, 0)


def permute(value, pairs):
    return lax.ppermute(value, "col", pairs)


def body(eigen_slab, secular_poles, coupling, window_roots, deflated, column_map):
    groups = lax.axis_size("col")
    row_groups = lax.axis_size("row")
    rows, cols_dev = eigen_slab.shape
    window = window_roots.shape[0]
    bits = log2(groups) - 1
    half = (lax.axis_index("row") >= row_groups // 2).astype(jnp.int32).reshape(1)
    me = lax.axis_index("col").astype(jnp.int32).reshape(1)
    tiled = lambda a: a.reshape(-1, LANES)
    rows_dev = cols_dev // LANES
    smem = pl.BlockSpec(memory_space=pltpu.SMEM)
    vmem = pl.BlockSpec(memory_space=pltpu.VMEM)
    hbm = pl.BlockSpec(memory_space=pltpu.HBM)
    mate = [(i, i ^ 1) for i in range(groups)]
    across = [[(i, partner(i, stage, bits)) for i in range(groups)] for stage in range(bits)]

    column_map, coupling, deflated, secular_poles = map(tiled, (column_map, coupling, deflated, secular_poles))
    listed = coupling.shape
    give, dense, live, poles, roots, slab_give = pl.pallas_call(
        functools.partial(place_kernel, groups=groups, cols_dev=cols_dev),
        out_shape=(
            pltpu.VMEM((groups // 2, 4 * rows_dev, LANES), F32),
            pltpu.VMEM((groups // 2, 4 * rows_dev, LANES), F32),
            pltpu.VMEM(listed, F32),
            pltpu.VMEM(listed, F32),
            pltpu.VMEM((1, window), F32),
            pltpu.VMEM((rows // 2, cols_dev), F32),
        ),
        in_specs=[smem] * 2 + [hbm] * 6,
        out_specs=(vmem,) * 6,
        scratch_shapes=[
            pltpu.VMEM(listed, jnp.int32),
            pltpu.VMEM(listed, F32),
            pltpu.VMEM(listed, jnp.int32),
            pltpu.SemaphoreType.DMA((5 + (1 << bits),)),
        ],
        name="place",
        compiler_params=PARAMS,
    )(
        half,
        me,
        *(
            pltpu.with_memory_space_constraint(a, pltpu.HBM)
            for a in (column_map, coupling, deflated, secular_poles, window_roots.reshape(1, window), eigen_slab)
        ),
    )

    term = pltpu.VMEM((rows // 2, cols_dev), BF16)
    own_terms = pl.pallas_call(
        functools.partial(fetch_split_kernel, bits=bits),
        out_shape=(term, term),
        in_specs=[smem, hbm],
        out_specs=(vmem, vmem),
        scratch_shapes=[pltpu.VMEM((rows // 2, cols_dev), F32), pltpu.SemaphoreType.DMA((1 << bits,))],
        name="fetch_split",
        compiler_params=PARAMS,
    )(me, pltpu.with_memory_space_constraint(eigen_slab, pltpu.HBM))
    squares, roots_t = pl.pallas_call(
        squares_kernel,
        out_shape=(pltpu.VMEM((SUBLANES, window), F32), pltpu.VMEM((window, LANES), F32)),
        in_specs=[vmem] * 3,
        out_specs=(vmem, vmem),
        name="sum_squares",
        compiler_params=PARAMS,
    )(roots, live, poles)

    value = dense + permute(give, mate)
    slab_got = permute(slab_give, mate)
    squares = squares + permute(squares, mate)
    for stage, pairs in enumerate(across, 1):
        mid = value.shape[0] // 2
        value = value[:mid] + permute(value[mid:], pairs)

    got_terms = pl.pallas_call(
        split_kernel,
        out_shape=(term, term),
        in_specs=[vmem],
        out_specs=(vmem, vmem),
        name="split_slab",
        compiler_params=PARAMS,
    )(slab_got)
    terms = (*own_terms, *got_terms)
    send, factor = pl.pallas_call(
        send_kernel,
        out_shape=(
            pltpu.VMEM((rows // 4 + SUBLANES, window), F32),
            pltpu.VMEM((2 * window, 2 * cols_dev), BF16),
        ),
        in_specs=[smem] + [vmem] * 7,
        out_specs=(vmem, vmem),
        name="send_rows",
        compiler_params=PARAMS,
    )(me, value.reshape(4 * rows_dev, LANES), roots_t, squares, *terms)
    keep = pl.pallas_call(
        keep_kernel,
        out_shape=pltpu.VMEM((rows // 4, window), F32),
        in_specs=[vmem] * 5,
        out_specs=vmem,
        name="keep_rows",
        compiler_params=PARAMS,
    )(factor, *terms)

    for stage, pairs in enumerate(across, 1):
        got = permute(send, pairs)
        mid = keep.shape[0]
        keep = keep + got[:mid]
        squares = squares + got[mid:]
        if stage < bits:
            keep, send = keep[: mid // 2], jnp.concatenate([keep[mid // 2 :], squares])
    return keep * lax.rsqrt(squares[:1])


def solution(mesh):
    return jax.shard_map(
        body,
        mesh=mesh,
        in_specs=(P("row", "col"), P("col"), P("col"), P(), P("col"), P("col")),
        out_specs=P(("row", "col"), None),
        check_vma=False,
    )
```
